256 devices in a mesh: outer: 16 (over z_hi, x, core), inner: 16 (over z_lo, y).
Axes of the slice: x: 4, y: 4, z: 8 (z_hi: 2, z_lo: 4; z = z_hi * 4 + z_lo), core: 2. Of those that a mesh axis runs over, the one named last changes fastest.
Arguments:
- tokens: bfloat16 [65536, 2048], P(('outer', 'inner')), may hold values from -6 to 6
- w_qkv: bfloat16 [2048, 3072], P('inner'), may hold values from -2.8 to 2.8
- w_out: bfloat16 [1024, 2048], P(None, 'inner'), may hold values from -1.5 to 1.5
- neighbours: int32 [256, 5], P(('outer', 'inner')), may hold values from -1 to 255, as said below
- counts: int32 [256], replicated, may hold values from 1 to 256, as said below
Outputs:
- attended: bfloat16 [65536, 2048], P(('outer', 'inner'))
The draws below stay inside these ranges and needn't reach their ends.
Inputs may be any that keep to these rules, and one draw needn't show every extreme that they name: `neighbours`: slot 0 of row b is b itself; slots 1 and 2 are the blocks b - 16 and b + 16 (the same inner index in the previous and next slab of outer), slots 3 and 4 the blocks b - 1 and b + 1 of the same slab; a slot holds -1 where its block lies outside the grid of blocks, and may hold -1 otherwise. `counts`: some block is full.
All inputs are finite; a program needn't handle non-finite values.
Results may differ from the reference program's by a relative error of at most 0.0093.
Values may be sent and summed in bfloat16 or wider, within the bound.
A program may use at most 64 MiB of HBM per device.

```python
import jax
import jax.numpy as jnp
from jax import lax

D = 2048
H = 8
HD = 128
NB = 5
BLK = 256
HH = 1024
BLOCKS = 256
TOKENS = 65536
N_OUTER = 16
N_INNER = 16


def draw_tokens(key, part):
    sample = jax.random.normal(key, (TOKENS, D), jnp.float32)
    return jnp.clip(sample, -6.0, 6.0).astype(jnp.bfloat16)


def draw_w_qkv(key, part):
    spread_value = D ** (-0.5)
    sample = jnp.clip(jax.random.normal(key, (D, 3 * HH), jnp.float32), -6.0, 6.0) * spread_value
    return jnp.clip(sample, -2.8, 2.8).astype(jnp.bfloat16)


def draw_neighbours(key, part):
    block_ids = jnp.arange(BLOCKS, dtype=jnp.int32)
    slab_no = block_ids // N_INNER
    inner_no = block_ids % N_INNER
    keeping = jax.random.randint(key, (BLOCKS, 4), 0, 4) > 0
    chosen = jnp.stack([block_ids - N_INNER, block_ids + N_INNER, block_ids - 1, block_ids + 1], axis=1)
    inside = jnp.stack([slab_no > 0, slab_no < N_OUTER - 1, inner_no > 0, inner_no < N_INNER - 1], axis=1)
    slots = jnp.where(inside & keeping, chosen, -1)
    return jnp.concatenate([block_ids[:, None], slots], axis=1).astype(jnp.int32)


def draw_counts(key, part):
    filled = jax.random.randint(key, (BLOCKS,), 1, BLK + 1)
    full_block = jax.random.randint(jax.random.fold_in(key, 7), (), 0, BLOCKS)
    return jnp.where(jnp.arange(BLOCKS) == full_block, BLK, filled).astype(jnp.int32)


def levels(key, shape, cuts, least, high):
    gain = 1.0
    for axis_at, blocks in cuts:
        heights = jax.random.uniform(jax.random.fold_in(jax.random.fold_in(key, 6), axis_at), (blocks,), jnp.float32, least / len(cuts), high / len(cuts))
        gain = gain * jnp.repeat(jnp.exp(heights), shape[axis_at] // blocks).reshape((-1,) + (1,) * (len(shape) - 1 - axis_at))
    return gain


def gaussian(key, shape, scale, most, pieces=(), kind=jnp.bfloat16):
    factor_of = levels(key, shape, pieces, -0.22, 0.18) if pieces else 1.0
    values = jax.random.normal(key, shape, jnp.float32) * scale * factor_of
    return jnp.minimum(jnp.maximum(values, -most), most).astype(kind)


def setup_inputs(seed: int = 0) -> dict:
    key_of = jax.random.split(jax.random.key(seed), 6)
    return {
        "tokens": draw_tokens(jax.random.fold_in(key_of[5], 71), 0),
        "w_qkv": draw_w_qkv(jax.random.fold_in(key_of[5], 71), 0),
        "w_out": gaussian(key_of[2], (HH, D), (HD // 8) ** -0.5, 1.5, ((1, 16),)),
        "neighbours": draw_neighbours(jax.random.fold_in(key_of[5], 71), 0),
        "counts": draw_counts(jax.random.fold_in(key_of[5], 71), 0),
    }


def normalize(values_in):
    values = values_in.astype(jnp.float32)
    center = values - lax.optimization_barrier(jnp.mean(values, axis=-1, keepdims=True))
    spread = lax.optimization_barrier(jnp.mean(center * center, axis=-1, keepdims=True))
    return (center * lax.rsqrt(spread + 1e-05)).astype(jnp.bfloat16)

def reference(tokens, w_qkv, w_out, neighbours, counts):
    normed = normalize(tokens)
    projected = jnp.dot(normed, w_qkv, preferred_element_type=jnp.float32).astype(jnp.bfloat16)
    grouped = projected.reshape(BLOCKS, BLK, 3 * HH)
    positions = jnp.arange(BLK, dtype=jnp.int32)
    score_scale = HD ** (-0.5)

    def attend(block_no):
        queries = grouped[block_no][:, :HH].astype(jnp.float32).reshape(BLK, H, HD)
        listed = neighbours[block_no]
        clipped = jnp.maximum(listed, 0).astype(jnp.int32)
        sources = grouped[clipped][:, :, HH:].astype(jnp.float32)
        keys_all = sources[:, :, :HH].reshape(NB, BLK, H, HD)
        values_all = sources[:, :, HH:].reshape(NB, BLK, H, HD)
        usable = (listed[:, None] >= 0) & (positions[None, :] < counts[clipped][:, None])
        scores = jnp.einsum('qhd,nkhd->hqnk', queries, keys_all) * score_scale
        masked = jnp.where(usable[None, None], scores, -jnp.inf)
        largest = lax.optimization_barrier(jnp.max(masked, axis=(2, 3), keepdims=True))
        weights = jnp.exp(masked - largest)
        totals = lax.optimization_barrier(jnp.sum(weights, axis=(2, 3)))
        rounded = lax.optimization_barrier(weights.astype(jnp.bfloat16)).astype(jnp.float32)
        context = jnp.einsum('hqnk,nkhd->qhd', rounded, values_all) / jnp.transpose(totals)[:, :, None]
        return context.reshape(BLK, HH).astype(jnp.bfloat16)
    context = lax.map(attend, jnp.arange(BLOCKS, dtype=jnp.int32))
    return jnp.dot(context.reshape(BLOCKS * BLK, HH), w_out, preferred_element_type=jnp.float32).astype(jnp.bfloat16)
```

```python
import functools
import math

import jax
import jax.numpy as jnp
from jax import lax
from jax.experimental import pallas as pl
from jax.experimental.pallas import tpu as pltpu
from jax.sharding import PartitionSpec as P

MESH = pl.DeviceIdType.MESH
HD = 128
EXP_SCALE = float(HD) ** (-0.5) * math.log2(math.e)
K, V, Q, O = 0, 1, 2, 3
SPLIT_X = {K: False, V: True, Q: True, O: False}
Z_FIRST = {K: True, V: True, Q: True, O: False}


def kernel(tokens, w_qkv, w_out, listed, counts, out, w, kv, queries, context, normed, tok, relay_buf,
           load_sem, tok_sem, recv_ring, send_ring, recv_mate, send_mate, recv_halo, send_halo, recv_relay, send_relay):
    o, i = lax.axis_index("outer"), lax.axis_index("inner")
    div, rem = lax.div, lax.rem
    x, c = rem(div(o, 2), 4), rem(o, 2)
    zl, y = div(i, 4), rem(i, 4)
    z = div(o, 8) * 4 + zl

    def dev(x, y, z, c):
        x, y, z = rem(x + 4, 4), rem(y + 4, 4), rem(z + 8, 8)
        return (div(z, 4) * 8 + x * 2 + c, rem(z, 4) * 4 + y)

    sign = 1 - 2 * c
    mate = dev(x, y, z, 1 - c)
    half = 4 * c
    outward_sign = 2 * c - 1
    outward = dev(x + outward_sign, y, z, 1 - c)
    is_edge = ((c == 0) & (x == 0)) | ((c == 1) & (x == 3))
    is_source = ((c == 0) & (z >= 4)) | ((c == 1) & (z < 4))
    edge_source = is_edge & is_source
    edge_end = is_edge & jnp.logical_not(is_source)
    inside = jnp.logical_not(is_edge)
    across_up = (y == 3) & (zl < 3)
    across_down = (y == 0) & (zl > 0)
    middle = (z >= 2) & (z <= 5)
    relay_sign = jnp.where(middle, 1, -1) * jnp.where(c == 0, 1, -1)
    relay_half = jnp.where(relay_sign > 0, 0, 1)

    loads = []

    def load_block(p, h, n):
        if p == O:
            src = w_out.at[pl.ds(pl.multiple_of(128 * h, 128), 128), :]
        else:
            base = {Q: 0, K: 1024, V: 2048}[p]
            src = w_qkv.at[:, pl.ds(pl.multiple_of(base + 128 * h, 128), 128)]
        copy = pltpu.make_async_copy(src, w.at[p, h, zl, y], load_sem.at[n])
        copy.start()
        return copy

    own_loads = {}
    number = 0
    for p in (V, K, Q, O):
        if SPLIT_X[p]:
            own_loads[p] = [load_block(p, half + x, number)]
            number += 1
        else:
            own_loads[p] = [load_block(p, half + j, number + j) for j in range(4)]
            number += 4
    tok_copy = pltpu.make_async_copy(tokens, tok, tok_sem)
    tok_copy.start()

    barrier = pltpu.get_barrier_semaphore()

    def greet(device):
        pl.semaphore_signal(barrier, inc=1, device_id=device, device_id_type=MESH)

    for device in (dev(x, y, z + 1, c), dev(x, y, z - 1, c), dev(x, y + 1, z, c), dev(x, y - 1, z, c),
                   dev(x + 1, y, z, c), dev(x - 1, y, z, c), mate):
        greet(device)

    @pl.when(inside)
    def _():
        greet(outward)

    @pl.when(is_edge)
    def _():
        for step in (2, -2):
            greet(dev(x + outward_sign, y, z + step, 1 - c))
            greet(dev(x, y, z + step, c))

    @pl.when(across_up)
    def _():
        greet(dev(x, 0, z + 1, c))

    @pl.when(across_down)
    def _():
        greet(dev(x, 3, z - 1, c))

    count = lambda pred: jnp.where(pred, 1, 0)
    pl.semaphore_wait(barrier, 8 + 3 * count(is_edge) + count(across_up) + count(across_down))

    sends = []

    def remote(src, dst, send, recv, device):
        return pltpu.make_async_remote_copy(
            src_ref=src, dst_ref=dst, send_sem=send, recv_sem=recv, device_id=device, device_id_type=MESH)

    def arrived(ref, recv):
        remote(ref, ref, send_mate.at[0, 0], recv, mate).wait_recv()

    def along(axis, step):
        return {"z": dev(x, y, z + step, c), "y": dev(x, y + step, z, c), "x": dev(x + step, y, z, c)}[axis]

    here = {"z": zl, "y": y, "x": x}

    def at(axis, step):
        return rem(here[axis] + step + 4, 4)

    def heads_of(p):
        return half + x if SPLIT_X[p] else pl.ds(half, 4)

    def first_axis(p):
        return "z" if Z_FIRST[p] else "y"

    def second_axis(p):
        return "y" if Z_FIRST[p] else "z"

    def ref_first(p, step):
        hs = heads_of(p)
        return w.at[p, hs, at("z", step), y] if Z_FIRST[p] else w.at[p, hs, zl, at("y", step)]

    def ref_second(p, step):
        hs = heads_of(p)
        return w.at[p, hs, :, at("y", step)] if Z_FIRST[p] else w.at[p, hs, at("z", step)]

    def ref_x(p, step):
        return w.at[p, half + at("x", step)]

    STAGES = {0: (ref_first, first_axis), 1: (ref_second, second_axis), 2: (ref_x, lambda p: "x")}

    def ring_send(p, stage, ref, slot, step):
        axis = STAGES[stage][1](p)
        copy = remote(ref, ref, send_ring.at[p, stage, slot], recv_ring.at[p, stage, slot], along(axis, step))
        copy.start()
        sends.append(copy)

    def ring_start(p, stage):
        ref = STAGES[stage][0](p, 0)
        ring_send(p, stage, ref, 0, 1)
        ring_send(p, stage, ref, 1, -1)

    def ring_relay(p, stage):
        ref = STAGES[stage][0](p, -sign)
        arrived(ref, recv_ring.at[p, stage, c])
        ring_send(p, stage, ref, 2, sign)
        return ref

    def ring_finish(p, stage):
        ref = STAGES[stage][0]
        a, b = ref(p, sign), ref(p, 2)
        arrived(a, recv_ring.at[p, stage, 1 - c])
        arrived(b, recv_ring.at[p, stage, 2])
        return a, b

    def to_mate(p, n, ref):
        copy = remote(ref, ref, send_mate.at[p, n], recv_mate.at[p, n], mate)
        copy.start()
        sends.append(copy)

    other = 4 * (1 - c)

    def from_mate(p):
        for n in range(4):
            if SPLIT_X[p]:
                step = {0: 0, 1: sign, 2: -sign, 3: 2}[n]
                ref = w.at[p, other + rem(x + step + 4, 4)]
            else:
                step = {0: 0, 1: sign, 2: -sign, 3: 2}[n]
                axis = second_axis(p)
                ref = (w.at[p, pl.ds(other, 4), :, at("y", step)] if axis == "y"
                       else w.at[p, pl.ds(other, 4), at("z", step)])
            arrived(ref, recv_mate.at[p, n])

    def first_start(p):
        for copy in own_loads[p]:
            copy.wait()
        ring_start(p, 0)

    def first_relay(p):
        ring_relay(p, 0)

    def second_start(p):
        ring_finish(p, 0)
        ring_start(p, 1)
        if not SPLIT_X[p]:
            to_mate(p, 0, ref_second(p, 0))

    def second_relay(p):
        ref = ring_relay(p, 1)
        if not SPLIT_X[p]:
            to_mate(p, 1, ref)

    def second_finish(p):
        a, b = ring_finish(p, 1)
        if SPLIT_X[p]:
            ring_start(p, 2)
            to_mate(p, 0, ref_x(p, 0))
        else:
            to_mate(p, 2, a)
            to_mate(p, 3, b)

    def x_relay(p):
        to_mate(p, 1, ring_relay(p, 2))

    def x_finish(p):
        a, b = ring_finish(p, 2)
        to_mate(p, 2, a)
        to_mate(p, 3, b)

    def normalize():
        tok_copy.wait()

        def body(n, _):
            rows = pl.ds(pl.multiple_of(n * 32, 32), 32)
            values = tok[rows, :].astype(jnp.float32)
            center = values - jnp.mean(values, axis=-1, keepdims=True)
            spread = jnp.mean(center * center, axis=-1, keepdims=True)
            normed[rows, :] = (center * lax.rsqrt(spread + 1e-05)).astype(jnp.bfloat16)
            return 0

        lax.fori_loop(0, 8, body, 0)

    def pair_of(p, h):
        return jnp.concatenate([w[p, h].reshape(2048, 128), w[p, h + 1].reshape(2048, 128)], axis=1)

    def project(p, first):
        def body(j, _):
            h = first + 2 * j
            result = jnp.dot(normed[...], pair_of(p, h), preferred_element_type=jnp.float32).astype(jnp.bfloat16)
            for k in range(2):
                part = result[:, 128 * k:128 * (k + 1)]
                if p == Q:
                    queries[h + k] = part
                else:
                    kv[0, h + k, p] = part
            return 0

        lax.fori_loop(0, 2, body, 0)

    def group(slot, g):
        return kv.at[slot, pl.ds(2 * g, 2)]

    cond_sends = []

    def when_send(pred, copy):
        @pl.when(pred)
        def _():
            copy.start()
        cond_sends.append((pred, copy))

    def local(slot, g):
        return pltpu.make_async_copy(group(0, g), group(slot, g), recv_halo.at[slot - 1, g])

    def halo_send(g):
        src = group(0, g)
        copy = remote(src, group(1 + c, g), send_halo.at[0, g], recv_halo.at[c, g], mate)
        copy.start()
        sends.append(copy)
        when_send(inside, remote(src, group(2 - c, g), send_halo.at[1, g], recv_halo.at[1 - c, g], outward))
        step = 2 if g % 2 == 0 else -2
        when_send(edge_source, remote(src, relay_buf.at[g // 2], send_halo.at[1, g], recv_relay.at[g // 2],
                                      dev(x + outward_sign, y, z + step, 1 - c)))

        @pl.when(edge_end)
        def _():
            local(1 + c, g).start()

        up, down = (o, jnp.minimum(i + 1, 15)), (o, jnp.maximum(i - 1, 0))
        when_send(i < 15, remote(src, group(3, g), send_halo.at[2, g], recv_halo.at[2, g], up))
        when_send(i > 0, remote(src, group(4, g), send_halo.at[3, g], recv_halo.at[3, g], down))

        @pl.when(i == 15)
        def _():
            local(4, g).start()

        @pl.when(i == 0)
        def _():
            local(3, g).start()

    def halo_relay():
        @pl.when(is_edge)
        def _():
            for k in range(2):
                arrived(relay_buf.at[k], recv_relay.at[k])
                g = 2 * k + relay_half
                remote(relay_buf.at[k], group(1 + c, g), send_relay.at[k], recv_halo.at[c, g],
                       dev(x, y, z + 2 * relay_sign, c)).start()

    def halo_relay_end():
        @pl.when(is_edge)
        def _():
            for k in range(2):
                g = 2 * k + relay_half
                remote(relay_buf.at[k], group(1 + c, g), send_relay.at[k], recv_halo.at[c, g],
                       dev(x, y, z + 2 * relay_sign, c)).wait_send()

    ids = lax.broadcasted_iota(jnp.int32, (1, 256), 1)
    masks = []
    for n in range(5):
        one = listed[0:1, n:n + 1]
        length = jnp.sum(jnp.where(ids == jnp.maximum(one, 0), counts[...], 0), axis=1, keepdims=True)
        masks.append(jnp.where((one >= 0) & (ids < length), 0.0, -jnp.inf).astype(jnp.float32))

    def attend(h):
        query = queries[h]
        scores = []
        for n in range(5):
            s = lax.dot_general(query, kv[n, h, 0], (((1,), (1,)), ((), ())), preferred_element_type=jnp.float32)
            scores.append(s + masks[n])
        top = scores[0]
        for n in range(1, 5):
            top = jnp.maximum(top, scores[n])
        largest = jnp.max(top, axis=1, keepdims=True)
        total = None
        acc = None
        for n in range(5):
            weight = jnp.exp2((scores[n] - largest) * EXP_SCALE)
            total = weight if total is None else total + weight
            part = jnp.dot(weight.astype(jnp.bfloat16), kv[n, h, 1], preferred_element_type=jnp.float32)
            acc = part if acc is None else acc + part
        totals = jnp.sum(total, axis=1, keepdims=True)
        context[:, pl.ds(pl.multiple_of(128 * h, 128), 128)] = (acc / totals).astype(jnp.bfloat16)

    def attention_group(g, _):
        for slot in range(1, 5):
            arrived(kv.at[slot, pl.ds(2 * g, 2)], recv_halo.at[slot - 1, g])

        def body(k, _):
            attend(2 * g + k)
            return 0

        lax.fori_loop(0, 2, body, 0)
        return 0

    def out_project():
        def body(n, _):
            zz, yy = div(n, 2), 2 * rem(n, 2)
            weights = jnp.concatenate(
                [w[O, :, zz, yy].reshape(1024, 128), w[O, :, zz, yy + 1].reshape(1024, 128)], axis=1)
            result = jnp.dot(context[...], weights, preferred_element_type=jnp.float32)
            out[:, pl.ds(pl.multiple_of(n * 256, 256), 256)] = result.astype(jnp.bfloat16)
            return 0

        lax.fori_loop(0, 8, body, 0)

    for p in (V, K, Q, O):
        first_start(p)
    first_relay(V)
    first_relay(K)
    second_start(V)
    second_start(K)
    first_relay(Q)
    first_relay(O)
    normalize()
    second_relay(V)
    second_finish(V)
    second_start(Q)
    second_start(O)
    second_relay(K)
    x_relay(V)
    second_relay(Q)
    second_finish(K)
    second_finish(Q)
    project(K, half)
    x_finish(V)
    project(V, half)
    from_mate(K)
    project(K, other)
    from_mate(V)
    project(V, other)
    for g in range(4):
        halo_send(g)
    second_relay(O)
    x_relay(Q)
    second_finish(O)
    x_finish(Q)
    project(Q, half)
    from_mate(Q)
    project(Q, other)
    halo_relay()
    lax.fori_loop(0, 4, attention_group, 0)
    from_mate(O)
    out_project()
    for copy in sends:
        copy.wait_send()
    for pred, copy in cond_sends:
        @pl.when(pred)
        def _(copy=copy):
            copy.wait_send()
    halo_relay_end()


def per_device(tokens, w_qkv, w_out, neighbours, counts):
    dma = pltpu.SemaphoreType.DMA
    vmem, hbm = pl.BlockSpec(memory_space=pltpu.VMEM), pl.BlockSpec(memory_space=pl.ANY)
    bf16 = jnp.bfloat16
    return pl.pallas_call(
        kernel,
        out_shape=jax.ShapeDtypeStruct((256, 2048), bf16),
        in_specs=[hbm, hbm, hbm, vmem, vmem],
        out_specs=vmem,
        scratch_shapes=[
            pltpu.VMEM((4, 8, 4, 4, 128, 128), bf16),
            pltpu.VMEM((5, 8, 2, 256, 128), bf16),
            pltpu.VMEM((8, 256, 128), bf16),
            pltpu.VMEM((256, 1024), bf16),
            pltpu.VMEM((256, 2048), bf16),
            pltpu.VMEM((256, 2048), bf16),
            pltpu.VMEM((2, 2, 2, 256, 128), bf16),
            dma((10,)), dma,
            dma((4, 3, 3)), dma((4, 3, 3)),
            dma((4, 4)), dma((4, 4)),
            dma((4, 4)), dma((4, 4)),
            dma((2,)), dma((2,)),
        ],
        compiler_params=pltpu.CompilerParams(
            collective_id=0, has_side_effects=True, vmem_limit_bytes=60 << 20),
    )(tokens, w_qkv, w_out, neighbours, counts.reshape(1, 256))


def solution(mesh):
    placed = (P(("outer", "inner"), None), P("inner", None), P(None, "inner"), P(("outer", "inner"), None), P())
    return jax.shard_map(
        per_device, mesh=mesh, in_specs=placed, out_specs=P(("outer", "inner"), None), check_vma=False)
```

```python
import math

import jax
import jax.numpy as jnp
from jax import lax
from jax.experimental import pallas as pl
from jax.experimental.pallas import tpu as pltpu
from jax.sharding import PartitionSpec as P

MESH = pl.DeviceIdType.MESH
HD = 128
EXP_SCALE = float(HD) ** (-0.5) * math.log2(math.e)
Q, K, V, O0, O1 = 0, 1, 2, 3, 4
Z_FIRST = {Q: True, K: True, V: False, O0: True, O1: False}
CHUNKS = 2
ROWS = 256 // CHUNKS


def kernel(tokens, w_qkv, w_out, listed, counts, out, wh, wo, raw, normed, queries, kv, above, below, masks, ctx_out, ctx,
           load_sem, tok_sem, recv_ring, send_ring, recv_mate, send_mate, recv_tok, send_tok, recv_tmate, send_tmate,
           recv_mask, send_mask, recv_up, recv_down, send_up, send_down, recv_edge, send_edge, recv_ctx, send_ctx):
    o, i = lax.axis_index("outer"), lax.axis_index("inner")
    div, rem = lax.div, lax.rem
    x, c = rem(div(o, 2), 4), rem(o, 2)
    zl, y = div(i, 4), rem(i, 4)
    zh = div(o, 8)
    z = zh * 4 + zl
    me = 2 * x + c

    def dev(x, y, z, c):
        x, y, z = rem(x + 4, 4), rem(y + 4, 4), rem(z + 8, 8)
        return (div(z, 4) * 8 + x * 2 + c, rem(z, 4) * 4 + y)

    def owner(j):
        return (zh * 8 + j, i)

    sign = 1 - 2 * c
    mate = dev(x, y, z, 1 - c)
    half, other = 4 * c, 4 * (1 - c)
    across_up = (y == 3) & (zl < 3)
    across_down = (y == 0) & (zl > 0)

    tok_copy = pltpu.make_async_copy(tokens, raw, tok_sem)
    tok_copy.start()
    own_loads = {}
    for p in (K, V, Q):
        src = w_qkv.at[:, pl.ds(pl.multiple_of(1024 * p + 128 * me, 128), 128)]
        own_loads[p] = [pltpu.make_async_copy(src, wh.at[p, zl, y], load_sem.at[p])]
    for p in (O0, O1):
        own_loads[p] = []
        for k in range(2):
            r = half + 2 * (p - O0) + k
            src = w_out.at[pl.ds(pl.multiple_of(128 * r, 128), 128), :]
            own_loads[p].append(pltpu.make_async_copy(src, wo.at[r, zl, y], load_sem.at[3 + 2 * (p - O0) + k]))
    for copies in own_loads.values():
        for copy in copies:
            copy.start()

    barrier = pltpu.get_barrier_semaphore()

    def greet(device):
        pl.semaphore_signal(barrier, inc=1, device_id=device, device_id_type=MESH)

    peers = [owner(rem(me + k, 8)) for k in range(1, 8)]
    peers += [dev(x, y, z + 1, c), dev(x, y, z - 1, c), dev(x, y + 1, z, c), dev(x, y - 1, z, c),
              dev(x, y, z + 2, c), dev(x, y, z - 2, c), dev(x, y + 2, z, c), dev(x, y, z + 4, c)]
    for device in peers:
        greet(device)

    @pl.when(across_up)
    def _():
        greet(dev(x, 0, z + 1, c))

    @pl.when(across_down)
    def _():
        greet(dev(x, 3, z - 1, c))

    tok_copy.wait()

    def normalize(n, _):
        rows = pl.ds(pl.multiple_of(n * 32, 32), 32)
        values = raw[rows, :].astype(jnp.float32)
        center = values - jnp.mean(values, axis=-1, keepdims=True)
        spread = jnp.mean(center * center, axis=-1, keepdims=True)
        normed[me, rows, :] = (center * lax.rsqrt(spread + 1e-05)).astype(jnp.bfloat16)
        return 0

    lax.fori_loop(0, 8, normalize, 0)

    ids = lax.broadcasted_iota(jnp.int32, (1, 256), 1)
    for n in range(5):
        one = listed[0:1, n:n + 1]
        length = jnp.sum(jnp.where(ids == jnp.maximum(one, 0), counts[...], 0), axis=1, keepdims=True)
        masks[me, n:n + 1, :] = jnp.where((one >= 0) & (ids < length), 0.0, -jnp.inf).astype(jnp.float32)

    zero = jnp.zeros((2, 256, 128), jnp.bfloat16)
    kv[9 * zh] = zero

    @pl.when(i == 15)
    def _():
        def fill(n, _):
            above[n] = zero
            return 0
        lax.fori_loop(0, 8, fill, 0)

    @pl.when(i == 0)
    def _():
        def fill(n, _):
            below[n] = zero
            return 0
        lax.fori_loop(0, 8, fill, 0)

    def count(pred):
        return jnp.where(pred, 1, 0)

    pl.semaphore_wait(barrier, len(peers) + count(across_up) + count(across_down))

    sends = []

    def remote(src, dst, send, recv, device):
        return pltpu.make_async_remote_copy(
            src_ref=src, dst_ref=dst, send_sem=send, recv_sem=recv, device_id=device, device_id_type=MESH)

    def go(src, dst, send, recv, device):
        copy = remote(src, dst, send, recv, device)
        copy.start()
        sends.append(copy)

    def arrived(ref, recv):
        remote(ref, ref, send_mate.at[0, 0], recv, mate).wait_recv()

    here = {"z": zl, "y": y}

    def at(axis, step):
        return rem(here[axis] + step + 4, 4)

    def along(axis, step):
        return dev(x, y, z + step, c) if axis == "z" else dev(x, y + step, z, c)

    def piece(p):
        if p < O0:
            return wh.at[p]
        return wo.at[pl.ds(half + 2 * (p - O0), 2)]

    def block(p, zi, yi):
        return wh.at[p, zi, yi] if p < O0 else wo.at[pl.ds(half + 2 * (p - O0), 2), zi, yi]

    def axis_of(p, stage):
        return "z" if Z_FIRST[p] == (stage == 0) else "y"

    def part(p, stage, step):
        if stage == 0:
            return block(p, at("z", step), y) if Z_FIRST[p] else block(p, zl, at("y", step))
        return block(p, slice(None), at("y", step)) if Z_FIRST[p] else block(p, at("z", step), slice(None))

    def ring_send(p, stage, ref, slot, step):
        go(ref, ref, send_ring.at[p, stage, slot], recv_ring.at[p, stage, slot], along(axis_of(p, stage), step))

    def ring_start(p, stage, direct=False):
        ref = part(p, stage, 0)
        ring_send(p, stage, ref, 0, 1)
        ring_send(p, stage, ref, 1, -1)
        if direct:
            ring_send(p, stage, ref, 2, 2 * sign)

    def ring_relay(p, stage):
        ref = part(p, stage, -sign)
        arrived(ref, recv_ring.at[p, stage, c])
        ring_send(p, stage, ref, 2, sign)
        return ref

    def ring_finish(p, stage, direct=False):
        if direct:
            arrived(part(p, stage, -sign), recv_ring.at[p, stage, c])
        a, b = part(p, stage, sign), part(p, stage, 2)
        arrived(a, recv_ring.at[p, stage, 1 - c])
        arrived(b, recv_ring.at[p, stage, 2])
        return a, b

    def to_mate(p, n, ref):
        go(ref, ref, send_mate.at[p - O0, n], recv_mate.at[p - O0, n], mate)

    def from_mate(p):
        rows = pl.ds(other + 2 * (p - O0), 2)
        for n, step in ((0, 0), (1, sign), (2, -sign), (3, 2)):
            ref = (wo.at[rows, :, at("y", step)] if Z_FIRST[p] else wo.at[rows, at("z", step)])
            arrived(ref, recv_mate.at[p - O0, n])

    def first_start(p):
        for copy in own_loads[p]:
            copy.wait()
        ring_start(p, 0, p < O0)

    def second_start(p):
        ring_finish(p, 0, p < O0)
        ring_start(p, 1, p < O0)
        if p >= O0:
            to_mate(p, 0, part(p, 1, 0))

    def second_relay(p):
        to_mate(p, 1, ring_relay(p, 1))

    def second_finish(p):
        a, b = ring_finish(p, 1)
        to_mate(p, 2, a)
        to_mate(p, 3, b)

    def rows_of(j, n):
        return normed.at[j, pl.ds(n * ROWS, ROWS)]

    def slab(step, core):
        return 2 * rem(x + step + 4, 4) + core

    def tok_start():
        for n in range(CHUNKS):
            ref = rows_of(me, n)
            go(ref, ref, send_tok.at[0, n], recv_tok.at[0, n], dev(x + 1, y, z, c))
            go(ref, ref, send_tok.at[1, n], recv_tok.at[1, n], dev(x - 1, y, z, c))
            go(ref, ref, send_tmate.at[0, n], recv_tmate.at[0, n], mate)

    def tok_relay(n):
        ref = rows_of(slab(-sign, c), n)
        arrived(ref, recv_tok.at[c, n])
        go(ref, ref, send_tok.at[2, n], recv_tok.at[2, n], dev(x + sign, y, z, c))
        go(ref, ref, send_tmate.at[1, n], recv_tmate.at[1, n], mate)

    def tok_pass(n):
        ref = rows_of(slab(sign, c), n)
        arrived(ref, recv_tok.at[1 - c, n])
        go(ref, ref, send_tmate.at[2, n], recv_tmate.at[2, n], mate)

    def tok_last(n):
        ref = rows_of(slab(2, c), n)
        arrived(ref, recv_tok.at[2, n])
        go(ref, ref, send_tmate.at[3, n], recv_tmate.at[3, n], mate)

    def tok_mate(m):
        step = {0: 0, 1: sign, 2: -sign, 3: 2}[m]
        for n in range(CHUNKS):
            arrived(rows_of(slab(step, 1 - c), n), recv_tmate.at[m, n])

    conditional = []

    def when_go(pred, copy):
        @pl.when(pred)
        def _():
            copy.start()
        conditional.append((pred, copy))

    up, down = (o, jnp.minimum(i + 1, 15)), (o, jnp.maximum(i - 1, 0))
    edge_slab = 7 * (1 - zh)

    def project_kv(j):
        weights = jnp.concatenate([wh[K].reshape(2048, 128), wh[V].reshape(2048, 128)], axis=1)
        result = jnp.dot(normed[j], weights, preferred_element_type=jnp.float32).astype(jnp.bfloat16)
        kv[j + 1, 0] = result[:, :128]
        kv[j + 1, 1] = result[:, 128:]

    def halo_send(j):
        ref = kv.at[j + 1]
        when_go(i < 15, remote(ref, below.at[j], send_up.at[j], recv_down.at[j], up))
        when_go(i > 0, remote(ref, above.at[j], send_down.at[j], recv_up.at[j], down))
        when_go(j == edge_slab, remote(ref, kv.at[9 * zh], send_edge, recv_edge, dev(x, y, z + 4, c)))

    def project_q(j):
        queries[j] = jnp.dot(normed[j], wh[Q].reshape(2048, 128), preferred_element_type=jnp.float32).astype(jnp.bfloat16)

    def attend(j, target):
        @pl.when(i < 15)
        def _():
            arrived(above.at[j], recv_up.at[j])

        @pl.when(i > 0)
        def _():
            arrived(below.at[j], recv_down.at[j])

        @pl.when(j == edge_slab)
        def _():
            arrived(kv.at[9 * (1 - zh)], recv_edge)

        query = queries[j]
        pairs = (lambda n: kv[j + 1, n], lambda n: kv[j, n], lambda n: kv[j + 2, n], lambda n: below[j, n],
                 lambda n: above[j, n])
        scores = []
        for n in range(5):
            s = lax.dot_general(query, pairs[n](0), (((1,), (1,)), ((), ())), preferred_element_type=jnp.float32)
            scores.append(s + masks[j, n:n + 1, :])
        top = scores[0]
        for n in range(1, 5):
            top = jnp.maximum(top, scores[n])
        largest = jnp.max(top, axis=1, keepdims=True)
        total = None
        acc = None
        for n in range(5):
            weight = jnp.exp2((scores[n] - largest) * EXP_SCALE)
            total = weight if total is None else total + weight
            one = jnp.dot(weight.astype(jnp.bfloat16), pairs[n](1), preferred_element_type=jnp.float32)
            acc = one if acc is None else acc + one
        totals = jnp.sum(total, axis=1, keepdims=True)
        target[...] = (acc / totals).astype(jnp.bfloat16)

    def attend_send(j):
        attend(j, ctx_out.at[j])
        go(ctx_out.at[j], ctx.at[me], send_ctx.at[j], recv_ctx.at[me], owner(j))

    def out_project():
        left = jnp.concatenate([ctx[h] for h in range(8)], axis=1)

        def body(n, _):
            zz, yy = div(n, 2), 2 * rem(n, 2)
            weights = jnp.concatenate(
                [wo[:, zz, yy].reshape(1024, 128), wo[:, zz, yy + 1].reshape(1024, 128)], axis=1)
            result = jnp.dot(left, weights, preferred_element_type=jnp.float32)
            out[:, pl.ds(pl.multiple_of(n * 256, 256), 256)] = result.astype(jnp.bfloat16)
            return 0

        lax.fori_loop(0, 8, body, 0)

    own, pal = me, slab(0, 1 - c)
    near = [slab(-sign, c), slab(sign, 1 - c), slab(sign, c), slab(-sign, 1 - c)]
    far = [slab(2, c), slab(2, 1 - c)]

    def handle(j):
        project_kv(j)
        halo_send(j)

    tok_start()
    for k in range(1, 8):
        go(masks.at[me], masks.at[me], send_mask.at[k], recv_mask.at[me], owner(rem(me + k, 8)))
    for p in (K, V, Q, O0, O1):
        first_start(p)
    for p in (K, V, Q):
        second_start(p)
    for p in (O0, O1):
        ring_relay(p, 0)
    for p in (O0, O1):
        second_start(p)
    tok_relay(0)
    for p in (K, V):
        ring_finish(p, 1, True)
    handle(own)
    tok_mate(0)
    handle(pal)
    for n in range(1, CHUNKS):
        tok_relay(n)
    for n in range(CHUNKS):
        tok_pass(n)
    for p in (O0, O1):
        second_relay(p)
    ring_finish(Q, 1, True)
    handle(near[0])
    handle(near[2])
    tok_mate(1)
    handle(near[1])
    tok_mate(2)
    handle(near[3])
    for p in (O0, O1):
        second_finish(p)
    for n in range(CHUNKS):
        tok_last(n)
    project_q(own)
    project_q(pal)
    for k in range(1, 8):
        j = rem(me + k, 8)
        arrived(masks.at[j], recv_mask.at[j])
    attend(own, ctx.at[me])
    attend_send(pal)
    handle(far[0])
    tok_mate(3)
    handle(far[1])
    for j in near:
        project_q(j)
    for j in near:
        attend_send(j)
    for j in far:
        project_q(j)
    for j in far:
        attend_send(j)
    for p in (O0, O1):
        from_mate(p)
    for k in range(1, 8):
        j = rem(me + k, 8)
        arrived(ctx.at[j], recv_ctx.at[j])
    out_project()
    for copy in sends:
        copy.wait_send()
    for pred, copy in conditional:
        @pl.when(pred)
        def _(copy=copy):
            copy.wait_send()


def per_device(tokens, w_qkv, w_out, neighbours, counts):
    dma = pltpu.SemaphoreType.DMA
    vmem, hbm = pl.BlockSpec(memory_space=pltpu.VMEM), pl.BlockSpec(memory_space=pl.ANY)
    bf16 = jnp.bfloat16
    return pl.pallas_call(
        kernel,
        out_shape=jax.ShapeDtypeStruct((256, 2048), bf16),
        in_specs=[hbm, hbm, hbm, vmem, vmem],
        out_specs=vmem,
        scratch_shapes=[
            pltpu.VMEM((3, 4, 4, 128, 128), bf16),
            pltpu.VMEM((8, 4, 4, 128, 128), bf16),
            pltpu.VMEM((256, 2048), bf16),
            pltpu.VMEM((8, 256, 2048), bf16),
            pltpu.VMEM((8, 256, 128), bf16),
            pltpu.VMEM((10, 2, 256, 128), bf16),
            pltpu.VMEM((8, 2, 256, 128), bf16),
            pltpu.VMEM((8, 2, 256, 128), bf16),
            pltpu.VMEM((8, 8, 256), jnp.float32),
            pltpu.VMEM((8, 256, 128), bf16),
            pltpu.VMEM((8, 256, 128), bf16),
            dma((7,)), dma,
            dma((5, 2, 3)), dma((5, 2, 3)),
            dma((2, 4)), dma((2, 4)),
            dma((3, CHUNKS)), dma((3, CHUNKS)),
            dma((4, CHUNKS)), dma((4, CHUNKS)),
            dma((8,)), dma((8,)),
            dma((8,)), dma((8,)), dma((8,)), dma((8,)),
            dma, dma,
            dma((8,)), dma((8,)),
        ],
        compiler_params=pltpu.CompilerParams(
            collective_id=0, has_side_effects=True, vmem_limit_bytes=60 << 20),
    )(tokens, w_qkv, w_out, neighbours, counts.reshape(1, 256))


def solution(mesh):
    placed = (P(("outer", "inner"), None), P("inner", None), P(None, "inner"), P(("outer", "inner"), None), P())
    return jax.shard_map(
        per_device, mesh=mesh, in_specs=placed, out_specs=P(("outer", "inner"), None), check_vma=False)
```

```python
import math

import jax
import jax.numpy as jnp
from jax import lax
from jax.experimental import pallas as pl
from jax.experimental.pallas import tpu as pltpu
from jax.sharding import PartitionSpec as P

MESH = pl.DeviceIdType.MESH
HD = 128
EXP_SCALE = float(HD) ** (-0.5) * math.log2(math.e)
Q, K, V, O0, O1 = 0, 1, 2, 3, 4
Z_FIRST = {Q: True, K: True, V: False, O0: False, O1: False}
CHUNKS = 2
ROWS = 256 // CHUNKS


def kernel(tokens, w_qkv, w_out, listed, counts, out, wh, wo, raw, normed, queries, kv, above, below, masks, ctx_out, ctx,
           load_sem, tok_sem, recv_ring, send_ring, recv_mate, send_mate, recv_tok, send_tok, recv_tmate, send_tmate,
           recv_mask, send_mask, recv_up, recv_down, send_up, send_down, recv_edge, send_edge, recv_ctx, send_ctx,
           edge_buf, cross_buf, recv_half, send_half, recv_cross, send_cross):
    o, i = lax.axis_index("outer"), lax.axis_index("inner")
    div, rem = lax.div, lax.rem
    x, c = rem(div(o, 2), 4), rem(o, 2)
    zl, y = div(i, 4), rem(i, 4)
    zh = div(o, 8)
    z = zh * 4 + zl
    me = 2 * x + c

    def dev(x, y, z, c):
        x, y, z = rem(x + 4, 4), rem(y + 4, 4), rem(z + 8, 8)
        return (div(z, 4) * 8 + x * 2 + c, rem(z, 4) * 4 + y)

    def owner(j):
        return (zh * 8 + j, i)

    sign = 1 - 2 * c
    mate = dev(x, y, z, 1 - c)
    half, other = 4 * c, 4 * (1 - c)
    across_up = (y == 3) & (zl < 3)
    across_down = (y == 0) & (zl > 0)
    turn_up, turn_down = (c == 1) & across_up, (c == 1) & across_down
    corner_up, corner_down = (c == 1) & (y == 0) & (zl < 3), (c == 1) & (y == 3) & (zl > 0)

    tok_copy = pltpu.make_async_copy(tokens, raw, tok_sem)
    tok_copy.start()
    own_loads = {}
    for p in (K, V, Q):
        src = w_qkv.at[:, pl.ds(pl.multiple_of(1024 * p + 128 * me, 128), 128)]
        own_loads[p] = [pltpu.make_async_copy(src, wh.at[p, zl, y], load_sem.at[p])]
    for p in (O0, O1):
        own_loads[p] = []
        for k in range(2):
            r = half + 2 * (p - O0) + k
            src = w_out.at[pl.ds(pl.multiple_of(128 * r, 128), 128), :]
            own_loads[p].append(pltpu.make_async_copy(src, wo.at[r, zl, y], load_sem.at[3 + 2 * (p - O0) + k]))
    for copies in own_loads.values():
        for copy in copies:
            copy.start()

    barrier = pltpu.get_barrier_semaphore()

    def greet(device):
        pl.semaphore_signal(barrier, inc=1, device_id=device, device_id_type=MESH)

    peers = [owner(rem(me + k, 8)) for k in range(1, 8)]
    peers += [dev(x, y, z + 1, c), dev(x, y, z - 1, c), dev(x, y + 1, z, c), dev(x, y - 1, z, c),
              dev(x, y, z + 2, c), dev(x, y, z - 2, c), dev(x, y + 2, z, c)]
    for device in peers:
        greet(device)

    @pl.when(across_up)
    def _():
        greet(dev(x, 0, z + 1, c))

    @pl.when(across_down)
    def _():
        greet(dev(x, 3, z - 1, c))

    tok_copy.wait()

    def normalize(n, _):
        rows = pl.ds(pl.multiple_of(n * 32, 32), 32)
        values = raw[rows, :].astype(jnp.float32)
        center = values - jnp.mean(values, axis=-1, keepdims=True)
        spread = jnp.mean(center * center, axis=-1, keepdims=True)
        normed[me, rows, :] = (center * lax.rsqrt(spread + 1e-05)).astype(jnp.bfloat16)
        return 0

    lax.fori_loop(0, 8, normalize, 0)

    ids = lax.broadcasted_iota(jnp.int32, (1, 256), 1)
    for n in range(5):
        one = listed[0:1, n:n + 1]
        length = jnp.sum(jnp.where(ids == jnp.maximum(one, 0), counts[...], 0), axis=1, keepdims=True)
        masks[me, n:n + 1, :] = jnp.where((one >= 0) & (ids < length), 0.0, -jnp.inf).astype(jnp.float32)

    zero = jnp.zeros((2, 256, 128), jnp.bfloat16)
    kv[9 * zh] = zero

    @pl.when(i == 15)
    def _():
        def fill(n, _):
            above[n] = zero
            return 0
        lax.fori_loop(0, 8, fill, 0)

    @pl.when(i == 0)
    def _():
        def fill(n, _):
            below[n] = zero
            return 0
        lax.fori_loop(0, 8, fill, 0)

    def count(pred):
        return jnp.where(pred, 1, 0)

    pl.semaphore_wait(barrier, len(peers) + count(across_up) + count(across_down))

    sends = []

    def remote(src, dst, send, recv, device):
        return pltpu.make_async_remote_copy(
            src_ref=src, dst_ref=dst, send_sem=send, recv_sem=recv, device_id=device, device_id_type=MESH)

    def go(src, dst, send, recv, device):
        copy = remote(src, dst, send, recv, device)
        copy.start()
        sends.append(copy)

    def arrived(ref, recv):
        remote(ref, ref, send_mate.at[0, 0], recv, mate).wait_recv()

    here = {"z": zl, "y": y}

    def at(axis, step):
        return rem(here[axis] + step + 4, 4)

    def along(axis, step):
        return dev(x, y, z + step, c) if axis == "z" else dev(x, y + step, z, c)

    def piece(p):
        if p < O0:
            return wh.at[p]
        return wo.at[pl.ds(half + 2 * (p - O0), 2)]

    def block(p, zi, yi):
        return wh.at[p, zi, yi] if p < O0 else wo.at[pl.ds(half + 2 * (p - O0), 2), zi, yi]

    def axis_of(p, stage):
        return "z" if Z_FIRST[p] == (stage == 0) else "y"

    def part(p, stage, step):
        if stage == 0:
            return block(p, at("z", step), y) if Z_FIRST[p] else block(p, zl, at("y", step))
        return block(p, slice(None), at("y", step)) if Z_FIRST[p] else block(p, at("z", step), slice(None))

    def ring_send(p, stage, ref, slot, step):
        go(ref, ref, send_ring.at[p, stage, slot], recv_ring.at[p, stage, slot], along(axis_of(p, stage), step))

    def ring_start(p, stage, direct=False):
        ref = part(p, stage, 0)
        ring_send(p, stage, ref, 0, 1)
        ring_send(p, stage, ref, 1, -1)
        if direct:
            ring_send(p, stage, ref, 2, 2 * sign)

    def ring_relay(p, stage):
        ref = part(p, stage, -sign)
        arrived(ref, recv_ring.at[p, stage, c])
        ring_send(p, stage, ref, 2, sign)
        return ref

    def ring_finish(p, stage, direct=False):
        if direct:
            arrived(part(p, stage, -sign), recv_ring.at[p, stage, c])
        a, b = part(p, stage, sign), part(p, stage, 2)
        arrived(a, recv_ring.at[p, stage, 1 - c])
        arrived(b, recv_ring.at[p, stage, 2])
        return a, b

    def to_mate(p, n, ref):
        go(ref, ref, send_mate.at[p - O0, n], recv_mate.at[p - O0, n], mate)

    def from_mate(p):
        rows = pl.ds(other + 2 * (p - O0), 2)
        for n, step in ((0, 0), (1, sign), (2, -sign), (3, 2)):
            ref = (wo.at[rows, :, at("y", step)] if Z_FIRST[p] else wo.at[rows, at("z", step)])
            arrived(ref, recv_mate.at[p - O0, n])

    def first_start(p):
        for copy in own_loads[p]:
            copy.wait()
        ring_start(p, 0, p < O0)

    def second_start(p):
        ring_finish(p, 0, p < O0)
        ring_start(p, 1)
        if p >= O0:
            to_mate(p, 0, part(p, 1, 0))

    def second_relay(p):
        to_mate(p, 1, ring_relay(p, 1))

    def second_finish(p):
        a, b = ring_finish(p, 1)
        to_mate(p, 2, a)
        to_mate(p, 3, b)

    def rows_of(j, n):
        return normed.at[j, pl.ds(n * ROWS, ROWS)]

    def slab(step, core):
        return 2 * rem(x + step + 4, 4) + core

    def tok_start():
        for n in range(CHUNKS):
            ref = rows_of(me, n)
            go(ref, ref, send_tok.at[0, n], recv_tok.at[0, n], dev(x + 1, y, z, c))
            go(ref, ref, send_tok.at[1, n], recv_tok.at[1, n], dev(x - 1, y, z, c))
            go(ref, ref, send_tmate.at[0, n], recv_tmate.at[0, n], mate)

    def tok_relay(n):
        ref = rows_of(slab(-sign, c), n)
        arrived(ref, recv_tok.at[c, n])
        go(ref, ref, send_tok.at[2, n], recv_tok.at[2, n], dev(x + sign, y, z, c))
        go(ref, ref, send_tmate.at[1, n], recv_tmate.at[1, n], mate)

    def tok_pass(n):
        ref = rows_of(slab(sign, c), n)
        arrived(ref, recv_tok.at[1 - c, n])
        go(ref, ref, send_tmate.at[2, n], recv_tmate.at[2, n], mate)

    def tok_last(n):
        ref = rows_of(slab(2, c), n)
        arrived(ref, recv_tok.at[2, n])
        go(ref, ref, send_tmate.at[3, n], recv_tmate.at[3, n], mate)

    def tok_mate(m):
        step = {0: 0, 1: sign, 2: -sign, 3: 2}[m]
        for n in range(CHUNKS):
            arrived(rows_of(slab(step, 1 - c), n), recv_tmate.at[m, n])

    conditional = []

    def when_go(pred, copy):
        @pl.when(pred)
        def _():
            copy.start()
        conditional.append((pred, copy))

    up, down = (o, jnp.minimum(i + 1, 15)), (o, jnp.maximum(i - 1, 0))
    edge_slab = 7 * (1 - zh)

    def project_kv(j):
        weights = jnp.concatenate([wh[K].reshape(2048, 128), wh[V].reshape(2048, 128)], axis=1)
        result = jnp.dot(normed[j], weights, preferred_element_type=jnp.float32).astype(jnp.bfloat16)
        kv[j + 1, 0] = result[:, :128]
        kv[j + 1, 1] = result[:, 128:]

    def halo_send(j):
        ref = kv.at[j + 1]
        when_go((i < 15) & jnp.logical_not(turn_up), remote(ref, below.at[j], send_up.at[j], recv_down.at[j], up))
        when_go((i > 0) & jnp.logical_not(turn_down), remote(ref, above.at[j], send_down.at[j], recv_up.at[j], down))
        when_go(turn_up, remote(ref, cross_buf.at[j], send_up.at[j], recv_cross.at[j], dev(x, y + 1, z, c)))
        when_go(turn_down, remote(ref, cross_buf.at[j], send_down.at[j], recv_cross.at[j], dev(x, y - 1, z, c)))
        when_go(j == edge_slab, remote(ref, edge_buf, send_half, recv_half, dev(x, y, z + 2 * sign, c)))

    def cross_relay(j):
        ref = cross_buf.at[j]

        @pl.when(corner_up | corner_down)
        def _():
            arrived(ref, recv_cross.at[j])
        when_go(corner_up, remote(ref, below.at[j], send_cross.at[j], recv_down.at[j], dev(x, y, z + 1, c)))
        when_go(corner_down, remote(ref, above.at[j], send_cross.at[j], recv_up.at[j], dev(x, y, z - 1, c)))

    end = rem(z + 2 * sign + 8, 8)

    def edge_relay(pred):
        @pl.when(pred)
        def _():
            arrived(edge_buf, recv_half)
        when_go(pred, remote(edge_buf, kv.at[9 * (1 - div(end, 4))], send_edge, recv_edge, dev(x, y, end, c)))

    outer_x = (x == 0) | (x == 3)

    def project_q(j):
        queries[j] = jnp.dot(normed[j], wh[Q].reshape(2048, 128), preferred_element_type=jnp.float32).astype(jnp.bfloat16)

    def attend(j, target):
        @pl.when(i < 15)
        def _():
            arrived(above.at[j], recv_up.at[j])

        @pl.when(i > 0)
        def _():
            arrived(below.at[j], recv_down.at[j])

        @pl.when(j == edge_slab)
        def _():
            arrived(kv.at[9 * (1 - zh)], recv_edge)

        query = queries[j]
        pairs = (lambda n: kv[j + 1, n], lambda n: kv[j, n], lambda n: kv[j + 2, n], lambda n: below[j, n],
                 lambda n: above[j, n])
        scores = []
        for n in range(5):
            s = lax.dot_general(query, pairs[n](0), (((1,), (1,)), ((), ())), preferred_element_type=jnp.float32)
            scores.append(s + masks[j, n:n + 1, :])
        top = scores[0]
        for n in range(1, 5):
            top = jnp.maximum(top, scores[n])
        largest = jnp.max(top, axis=1, keepdims=True)
        total = None
        acc = None
        for n in range(5):
            weight = jnp.exp2((scores[n] - largest) * EXP_SCALE)
            total = weight if total is None else total + weight
            one = jnp.dot(weight.astype(jnp.bfloat16), pairs[n](1), preferred_element_type=jnp.float32)
            acc = one if acc is None else acc + one
        totals = jnp.sum(total, axis=1, keepdims=True)
        target[...] = (acc / totals).astype(jnp.bfloat16)

    def attend_send(j):
        attend(j, ctx_out.at[j])
        go(ctx_out.at[j], ctx.at[me], send_ctx.at[j], recv_ctx.at[me], owner(j))

    def out_project():
        left = jnp.concatenate([ctx[h] for h in range(8)], axis=1)

        def body(n, _):
            zz, yy = div(n, 2), 2 * rem(n, 2)
            weights = jnp.concatenate(
                [wo[:, zz, yy].reshape(1024, 128), wo[:, zz, yy + 1].reshape(1024, 128)], axis=1)
            result = jnp.dot(left, weights, preferred_element_type=jnp.float32)
            out[:, pl.ds(pl.multiple_of(n * 256, 256), 256)] = result.astype(jnp.bfloat16)
            return 0

        lax.fori_loop(0, 8, body, 0)

    own, pal = me, slab(0, 1 - c)
    near = [slab(-sign, c), slab(sign, 1 - c), slab(sign, c), slab(-sign, 1 - c)]
    far = [slab(2, c), slab(2, 1 - c)]

    def handle(j):
        project_kv(j)
        halo_send(j)

    tok_start()
    for k in range(1, 8):
        go(masks.at[me], masks.at[me], send_mask.at[k], recv_mask.at[me], owner(rem(me + k, 8)))
    for p in (K, V, Q, O0, O1):
        first_start(p)
    for p in (K, V, Q):
        second_start(p)
    for p in (O0, O1):
        ring_relay(p, 0)
    for p in (K, V, Q):
        ring_relay(p, 1)
    for p in (O0, O1):
        second_start(p)
    tok_relay(0)
    for p in (K, V):
        ring_finish(p, 1)
    handle(own)
    tok_mate(0)
    handle(pal)
    for n in range(1, CHUNKS):
        tok_relay(n)
    cross_relay(own)
    cross_relay(pal)
    for n in range(CHUNKS):
        tok_pass(n)
    for p in (O0, O1):
        second_relay(p)
    ring_finish(Q, 1)
    handle(near[0])
    handle(near[2])
    tok_mate(1)
    handle(near[1])
    tok_mate(2)
    handle(near[3])
    for p in (O0, O1):
        second_finish(p)
    project_q(own)
    project_q(pal)
    for j in (near[0], near[2], near[1], near[3]):
        cross_relay(j)
    edge_relay(outer_x)
    for n in range(CHUNKS):
        tok_last(n)
    for k in range(1, 8):
        j = rem(me + k, 8)
        arrived(masks.at[j], recv_mask.at[j])
    handle(far[0])
    tok_mate(3)
    handle(far[1])
    attend(own, ctx.at[me])
    attend_send(pal)
    edge_relay(jnp.logical_not(outer_x))
    for j in far:
        cross_relay(j)
    for j in near:
        project_q(j)
    for j in near:
        attend_send(j)
    for j in far:
        project_q(j)
    for j in far:
        attend_send(j)
    for p in (O0, O1):
        from_mate(p)
    for k in range(1, 8):
        j = rem(me + k, 8)
        arrived(ctx.at[j], recv_ctx.at[j])
    out_project()
    for copy in sends:
        copy.wait_send()
    for pred, copy in conditional:
        @pl.when(pred)
        def _(copy=copy):
            copy.wait_send()


def per_device(tokens, w_qkv, w_out, neighbours, counts):
    dma = pltpu.SemaphoreType.DMA
    vmem, hbm = pl.BlockSpec(memory_space=pltpu.VMEM), pl.BlockSpec(memory_space=pl.ANY)
    bf16 = jnp.bfloat16
    return pl.pallas_call(
        kernel,
        out_shape=jax.ShapeDtypeStruct((256, 2048), bf16),
        in_specs=[hbm, hbm, hbm, vmem, vmem],
        out_specs=vmem,
        scratch_shapes=[
            pltpu.VMEM((3, 4, 4, 128, 128), bf16),
            pltpu.VMEM((8, 4, 4, 128, 128), bf16),
            pltpu.VMEM((256, 2048), bf16),
            pltpu.VMEM((8, 256, 2048), bf16),
            pltpu.VMEM((8, 256, 128), bf16),
            pltpu.VMEM((10, 2, 256, 128), bf16),
            pltpu.VMEM((8, 2, 256, 128), bf16),
            pltpu.VMEM((8, 2, 256, 128), bf16),
            pltpu.VMEM((8, 8, 256), jnp.float32),
            pltpu.VMEM((8, 256, 128), bf16),
            pltpu.VMEM((8, 256, 128), bf16),
            dma((7,)), dma,
            dma((5, 2, 3)), dma((5, 2, 3)),
            dma((2, 4)), dma((2, 4)),
            dma((3, CHUNKS)), dma((3, CHUNKS)),
            dma((4, CHUNKS)), dma((4, CHUNKS)),
            dma((8,)), dma((8,)),
            dma((8,)), dma((8,)), dma((8,)), dma((8,)),
            dma, dma,
            dma((8,)), dma((8,)),
            pltpu.VMEM((2, 256, 128), bf16),
            pltpu.VMEM((8, 2, 256, 128), bf16),
            dma, dma,
            dma((8,)), dma((8,)),
        ],
        compiler_params=pltpu.CompilerParams(
            collective_id=0, has_side_effects=True, vmem_limit_bytes=60 << 20),
    )(tokens, w_qkv, w_out, neighbours, counts.reshape(1, 256))


def solution(mesh):
    placed = (P(("outer", "inner"), None), P("inner", None), P(None, "inner"), P(("outer", "inner"), None), P())
    return jax.shard_map(
        per_device, mesh=mesh, in_specs=placed, out_specs=P(("outer", "inner"), None), check_vma=False)
```

```python
import math

import jax
import jax.numpy as jnp
from jax import lax
from jax.experimental import pallas as pl
from jax.experimental.pallas import tpu as pltpu
from jax.sharding import PartitionSpec as P

MESH = pl.DeviceIdType.MESH
HD = 128
EXP_SCALE = float(HD) ** (-0.5) * math.log2(math.e)
Q, K, V, O0, O1 = 0, 1, 2, 3, 4
Z_FIRST = {Q: True, K: True, V: False, O0: False, O1: False}
CHUNKS = 2
ROWS = 256 // CHUNKS


def kernel(tokens, w_qkv, w_out, listed, counts, out, wh, wo, raw, normed, queries, kv, above, below, masks, ctx_out, ctx,
           load_sem, tok_sem, recv_ring, send_ring, recv_mate, send_mate, recv_tok, send_tok, recv_tmate, send_tmate,
           recv_mask, send_mask, recv_up, recv_down, send_up, send_down, recv_edge, send_edge, recv_ctx, send_ctx,
           cross_buf, recv_cross, send_cross):
    o, i = lax.axis_index("outer"), lax.axis_index("inner")
    div, rem = lax.div, lax.rem
    x, c = rem(div(o, 2), 4), rem(o, 2)
    zl, y = div(i, 4), rem(i, 4)
    zh = div(o, 8)
    z = zh * 4 + zl
    me = 2 * x + c

    def dev(x, y, z, c):
        x, y, z = rem(x + 4, 4), rem(y + 4, 4), rem(z + 8, 8)
        return (div(z, 4) * 8 + x * 2 + c, rem(z, 4) * 4 + y)

    def owner(j):
        return (zh * 8 + j, i)

    sign = 1 - 2 * c
    mate = dev(x, y, z, 1 - c)
    half, other = 4 * c, 4 * (1 - c)
    across_up = (y == 3) & (zl < 3)
    across_down = (y == 0) & (zl > 0)
    turn_up, turn_down = (c == 1) & across_up, (c == 1) & across_down
    corner_up, corner_down = (c == 1) & (y == 0) & (zl < 3), (c == 1) & (y == 3) & (zl > 0)

    tok_copy = pltpu.make_async_copy(tokens, raw, tok_sem)
    tok_copy.start()
    own_loads = {}
    for p in (K, V, Q):
        src = w_qkv.at[:, pl.ds(pl.multiple_of(1024 * p + 128 * me, 128), 128)]
        own_loads[p] = [pltpu.make_async_copy(src, wh.at[p, zl, y], load_sem.at[p])]
    for p in (O0, O1):
        own_loads[p] = []
        for k in range(2):
            r = half + 2 * (p - O0) + k
            src = w_out.at[pl.ds(pl.multiple_of(128 * r, 128), 128), :]
            own_loads[p].append(pltpu.make_async_copy(src, wo.at[r, zl, y], load_sem.at[3 + 2 * (p - O0) + k]))
    for copies in own_loads.values():
        for copy in copies:
            copy.start()

    barrier = pltpu.get_barrier_semaphore()

    def greet(device):
        pl.semaphore_signal(barrier, inc=1, device_id=device, device_id_type=MESH)

    peers = [owner(rem(me + k, 8)) for k in range(1, 8)]
    peers += [dev(x, y, z + 1, c), dev(x, y, z - 1, c), dev(x, y + 1, z, c), dev(x, y - 1, z, c),
              dev(x, y, z + 2, c), dev(x, y, z - 2, c), dev(x, y + 2, z, c), dev(x, y, z + 4, c)]
    for device in peers:
        greet(device)

    @pl.when(across_up)
    def _():
        greet(dev(x, 0, z + 1, c))

    @pl.when(across_down)
    def _():
        greet(dev(x, 3, z - 1, c))

    tok_copy.wait()

    def normalize(n, _):
        rows = pl.ds(pl.multiple_of(n * 32, 32), 32)
        values = raw[rows, :].astype(jnp.float32)
        center = values - jnp.mean(values, axis=-1, keepdims=True)
        spread = jnp.mean(center * center, axis=-1, keepdims=True)
        normed[me, rows, :] = (center * lax.rsqrt(spread + 1e-05)).astype(jnp.bfloat16)
        return 0

    lax.fori_loop(0, 8, normalize, 0)

    ids = lax.broadcasted_iota(jnp.int32, (1, 256), 1)
    for n in range(5):
        one = listed[0:1, n:n + 1]
        length = jnp.sum(jnp.where(ids == jnp.maximum(one, 0), counts[...], 0), axis=1, keepdims=True)
        masks[me, n:n + 1, :] = jnp.where((one >= 0) & (ids < length), 0.0, -jnp.inf).astype(jnp.float32)

    zero = jnp.zeros((2, 256, 128), jnp.bfloat16)
    kv[9 * zh] = zero

    @pl.when(i == 15)
    def _():
        def fill(n, _):
            above[n] = zero
            return 0
        lax.fori_loop(0, 8, fill, 0)

    @pl.when(i == 0)
    def _():
        def fill(n, _):
            below[n] = zero
            return 0
        lax.fori_loop(0, 8, fill, 0)

    def count(pred):
        return jnp.where(pred, 1, 0)

    pl.semaphore_wait(barrier, len(peers) + count(across_up) + count(across_down))

    sends = []

    def remote(src, dst, send, recv, device):
        return pltpu.make_async_remote_copy(
            src_ref=src, dst_ref=dst, send_sem=send, recv_sem=recv, device_id=device, device_id_type=MESH)

    def go(src, dst, send, recv, device):
        copy = remote(src, dst, send, recv, device)
        copy.start()
        sends.append(copy)

    def arrived(ref, recv):
        remote(ref, ref, send_mate.at[0, 0], recv, mate).wait_recv()

    here = {"z": zl, "y": y}

    def at(axis, step):
        return rem(here[axis] + step + 4, 4)

    def along(axis, step):
        return dev(x, y, z + step, c) if axis == "z" else dev(x, y + step, z, c)

    def piece(p):
        if p < O0:
            return wh.at[p]
        return wo.at[pl.ds(half + 2 * (p - O0), 2)]

    def block(p, zi, yi):
        return wh.at[p, zi, yi] if p < O0 else wo.at[pl.ds(half + 2 * (p - O0), 2), zi, yi]

    def axis_of(p, stage):
        return "z" if Z_FIRST[p] == (stage == 0) else "y"

    def part(p, stage, step):
        if stage == 0:
            return block(p, at("z", step), y) if Z_FIRST[p] else block(p, zl, at("y", step))
        return block(p, slice(None), at("y", step)) if Z_FIRST[p] else block(p, at("z", step), slice(None))

    def ring_send(p, stage, ref, slot, step):
        go(ref, ref, send_ring.at[p, stage, slot], recv_ring.at[p, stage, slot], along(axis_of(p, stage), step))

    def ring_start(p, stage, direct=False):
        ref = part(p, stage, 0)
        ring_send(p, stage, ref, 0, 1)
        ring_send(p, stage, ref, 1, -1)
        if direct:
            ring_send(p, stage, ref, 2, 2 * sign)

    def ring_relay(p, stage):
        ref = part(p, stage, -sign)
        arrived(ref, recv_ring.at[p, stage, c])
        ring_send(p, stage, ref, 2, sign)
        return ref

    def ring_finish(p, stage, direct=False):
        if direct:
            arrived(part(p, stage, -sign), recv_ring.at[p, stage, c])
        a, b = part(p, stage, sign), part(p, stage, 2)
        arrived(a, recv_ring.at[p, stage, 1 - c])
        arrived(b, recv_ring.at[p, stage, 2])
        return a, b

    def to_mate(p, n, ref):
        go(ref, ref, send_mate.at[p - O0, n], recv_mate.at[p - O0, n], mate)

    def from_mate(p):
        rows = pl.ds(other + 2 * (p - O0), 2)
        for n, step in ((0, 0), (1, sign), (2, -sign), (3, 2)):
            ref = (wo.at[rows, :, at("y", step)] if Z_FIRST[p] else wo.at[rows, at("z", step)])
            arrived(ref, recv_mate.at[p - O0, n])

    def first_start(p):
        for copy in own_loads[p]:
            copy.wait()
        ring_start(p, 0, p < O0)

    def second_start(p):
        ring_finish(p, 0, p < O0)
        ring_start(p, 1)
        if p >= O0:
            to_mate(p, 0, part(p, 1, 0))

    def second_relay(p):
        to_mate(p, 1, ring_relay(p, 1))

    def second_finish(p):
        a, b = ring_finish(p, 1)
        to_mate(p, 2, a)
        to_mate(p, 3, b)

    def rows_of(j, n):
        return normed.at[j, pl.ds(n * ROWS, ROWS)]

    def slab(step, core):
        return 2 * rem(x + step + 4, 4) + core

    def tok_start():
        for n in range(CHUNKS):
            ref = rows_of(me, n)
            go(ref, ref, send_tok.at[0, n], recv_tok.at[0, n], dev(x + 1, y, z, c))
            go(ref, ref, send_tok.at[1, n], recv_tok.at[1, n], dev(x - 1, y, z, c))
            go(ref, ref, send_tmate.at[0, n], recv_tmate.at[0, n], mate)

    def tok_relay(n):
        ref = rows_of(slab(-sign, c), n)
        arrived(ref, recv_tok.at[c, n])
        go(ref, ref, send_tok.at[2, n], recv_tok.at[2, n], dev(x + sign, y, z, c))
        go(ref, ref, send_tmate.at[1, n], recv_tmate.at[1, n], mate)

    def tok_pass(n):
        ref = rows_of(slab(sign, c), n)
        arrived(ref, recv_tok.at[1 - c, n])
        go(ref, ref, send_tmate.at[2, n], recv_tmate.at[2, n], mate)

    def tok_last(n):
        ref = rows_of(slab(2, c), n)
        arrived(ref, recv_tok.at[2, n])
        go(ref, ref, send_tmate.at[3, n], recv_tmate.at[3, n], mate)

    def tok_mate(m):
        step = {0: 0, 1: sign, 2: -sign, 3: 2}[m]
        for n in range(CHUNKS):
            arrived(rows_of(slab(step, 1 - c), n), recv_tmate.at[m, n])

    conditional = []

    def when_go(pred, copy):
        @pl.when(pred)
        def _():
            copy.start()
        conditional.append((pred, copy))

    up, down = (o, jnp.minimum(i + 1, 15)), (o, jnp.maximum(i - 1, 0))
    edge_slab = 7 * (1 - zh)

    def project_kv(j):
        weights = jnp.concatenate([wh[K].reshape(2048, 128), wh[V].reshape(2048, 128)], axis=1)
        result = jnp.dot(normed[j], weights, preferred_element_type=jnp.float32).astype(jnp.bfloat16)
        kv[j + 1, 0] = result[:, :128]
        kv[j + 1, 1] = result[:, 128:]

    def halo_send(j):
        ref = kv.at[j + 1]
        when_go((i < 15) & jnp.logical_not(turn_up), remote(ref, below.at[j], send_up.at[j], recv_down.at[j], up))
        when_go((i > 0) & jnp.logical_not(turn_down), remote(ref, above.at[j], send_down.at[j], recv_up.at[j], down))
        when_go(turn_up, remote(ref, cross_buf.at[j], send_up.at[j], recv_cross.at[j], dev(x, y + 1, z, c)))
        when_go(turn_down, remote(ref, cross_buf.at[j], send_down.at[j], recv_cross.at[j], dev(x, y - 1, z, c)))
        when_go(j == edge_slab, remote(ref, kv.at[9 * zh], send_edge, recv_edge, dev(x, y, z + 4, c)))

    def cross_relay(j):
        ref = cross_buf.at[j]

        @pl.when(corner_up | corner_down)
        def _():
            arrived(ref, recv_cross.at[j])
        when_go(corner_up, remote(ref, below.at[j], send_cross.at[j], recv_down.at[j], dev(x, y, z + 1, c)))
        when_go(corner_down, remote(ref, above.at[j], send_cross.at[j], recv_up.at[j], dev(x, y, z - 1, c)))

    def project_q(j):
        queries[j] = jnp.dot(normed[j], wh[Q].reshape(2048, 128), preferred_element_type=jnp.float32).astype(jnp.bfloat16)

    def attend(j, target):
        @pl.when(i < 15)
        def _():
            arrived(above.at[j], recv_up.at[j])

        @pl.when(i > 0)
        def _():
            arrived(below.at[j], recv_down.at[j])

        @pl.when(j == edge_slab)
        def _():
            arrived(kv.at[9 * (1 - zh)], recv_edge)

        query = queries[j]
        pairs = (lambda n: kv[j + 1, n], lambda n: kv[j, n], lambda n: kv[j + 2, n], lambda n: below[j, n],
                 lambda n: above[j, n])
        scores = []
        for n in range(5):
            s = lax.dot_general(query, pairs[n](0), (((1,), (1,)), ((), ())), preferred_element_type=jnp.float32)
            scores.append(s + masks[j, n:n + 1, :])
        top = scores[0]
        for n in range(1, 5):
            top = jnp.maximum(top, scores[n])
        largest = jnp.max(top, axis=1, keepdims=True)
        total = None
        acc = None
        for n in range(5):
            weight = jnp.exp2((scores[n] - largest) * EXP_SCALE)
            total = weight if total is None else total + weight
            one = jnp.dot(weight.astype(jnp.bfloat16), pairs[n](1), preferred_element_type=jnp.float32)
            acc = one if acc is None else acc + one
        totals = jnp.sum(total, axis=1, keepdims=True)
        target[...] = (acc / totals).astype(jnp.bfloat16)

    def attend_send(j):
        attend(j, ctx_out.at[j])
        go(ctx_out.at[j], ctx.at[me], send_ctx.at[j], recv_ctx.at[me], owner(j))

    def out_project():
        left = jnp.concatenate([ctx[h] for h in range(8)], axis=1)

        def body(n, _):
            zz, yy = div(n, 2), 2 * rem(n, 2)
            weights = jnp.concatenate(
                [wo[:, zz, yy].reshape(1024, 128), wo[:, zz, yy + 1].reshape(1024, 128)], axis=1)
            result = jnp.dot(left, weights, preferred_element_type=jnp.float32)
            out[:, pl.ds(pl.multiple_of(n * 256, 256), 256)] = result.astype(jnp.bfloat16)
            return 0

        lax.fori_loop(0, 8, body, 0)

    own, pal = me, slab(0, 1 - c)
    near = [slab(-sign, c), slab(sign, 1 - c), slab(sign, c), slab(-sign, 1 - c)]
    far = [slab(2, c), slab(2, 1 - c)]

    def handle(j):
        project_kv(j)
        halo_send(j)

    tok_start()
    for k in range(1, 8):
        go(masks.at[me], masks.at[me], send_mask.at[k], recv_mask.at[me], owner(rem(me + k, 8)))
    for p in (K, V, Q, O0, O1):
        first_start(p)
    for p in (K, V, Q):
        second_start(p)
    for p in (O0, O1):
        ring_relay(p, 0)
    for p in (K, V, Q):
        ring_relay(p, 1)
    for p in (O0, O1):
        second_start(p)
    tok_relay(0)
    for p in (K, V):
        ring_finish(p, 1)
    handle(own)
    tok_mate(0)
    handle(pal)
    for n in range(1, CHUNKS):
        tok_relay(n)
    cross_relay(own)
    cross_relay(pal)
    for n in range(CHUNKS):
        tok_pass(n)
    for p in (O0, O1):
        second_relay(p)
    ring_finish(Q, 1)
    handle(near[0])
    handle(near[2])
    tok_mate(1)
    handle(near[1])
    tok_mate(2)
    handle(near[3])
    for p in (O0, O1):
        second_finish(p)
    project_q(own)
    project_q(pal)
    for j in (near[0], near[2], near[1], near[3]):
        cross_relay(j)
    for n in range(CHUNKS):
        tok_last(n)
    for k in range(1, 8):
        j = rem(me + k, 8)
        arrived(masks.at[j], recv_mask.at[j])
    handle(far[0])
    tok_mate(3)
    handle(far[1])
    attend(own, ctx.at[me])
    attend_send(pal)
    for j in far:
        cross_relay(j)
    for j in near:
        project_q(j)
    for j in near:
        attend_send(j)
    for j in far:
        project_q(j)
    for j in far:
        attend_send(j)
    for p in (O0, O1):
        from_mate(p)
    for k in range(1, 8):
        j = rem(me + k, 8)
        arrived(ctx.at[j], recv_ctx.at[j])
    out_project()
    for copy in sends:
        copy.wait_send()
    for pred, copy in conditional:
        @pl.when(pred)
        def _(copy=copy):
            copy.wait_send()


def per_device(tokens, w_qkv, w_out, neighbours, counts):
    dma = pltpu.SemaphoreType.DMA
    vmem, hbm = pl.BlockSpec(memory_space=pltpu.VMEM), pl.BlockSpec(memory_space=pl.ANY)
    bf16 = jnp.bfloat16
    return pl.pallas_call(
        kernel,
        out_shape=jax.ShapeDtypeStruct((256, 2048), bf16),
        in_specs=[hbm, hbm, hbm, vmem, vmem],
        out_specs=vmem,
        scratch_shapes=[
            pltpu.VMEM((3, 4, 4, 128, 128), bf16),
            pltpu.VMEM((8, 4, 4, 128, 128), bf16),
            pltpu.VMEM((256, 2048), bf16),
            pltpu.VMEM((8, 256, 2048), bf16),
            pltpu.VMEM((8, 256, 128), bf16),
            pltpu.VMEM((10, 2, 256, 128), bf16),
            pltpu.VMEM((8, 2, 256, 128), bf16),
            pltpu.VMEM((8, 2, 256, 128), bf16),
            pltpu.VMEM((8, 8, 256), jnp.float32),
            pltpu.VMEM((8, 256, 128), bf16),
            pltpu.VMEM((8, 256, 128), bf16),
            dma((7,)), dma,
            dma((5, 2, 3)), dma((5, 2, 3)),
            dma((2, 4)), dma((2, 4)),
            dma((3, CHUNKS)), dma((3, CHUNKS)),
            dma((4, CHUNKS)), dma((4, CHUNKS)),
            dma((8,)), dma((8,)),
            dma((8,)), dma((8,)), dma((8,)), dma((8,)),
            dma, dma,
            dma((8,)), dma((8,)),
            pltpu.VMEM((8, 2, 256, 128), bf16),
            dma((8,)), dma((8,)),
        ],
        compiler_params=pltpu.CompilerParams(
            collective_id=0, has_side_effects=True, vmem_limit_bytes=60 << 20),
    )(tokens, w_qkv, w_out, neighbours, counts.reshape(1, 256))


def solution(mesh):
    placed = (P(("outer", "inner"), None), P("inner", None), P(None, "inner"), P(("outer", "inner"), None), P())
    return jax.shard_map(
        per_device, mesh=mesh, in_specs=placed, out_specs=P(("outer", "inner"), None), check_vma=False)
```

```python
import math

import jax
import jax.numpy as jnp
from jax import lax
from jax.experimental import pallas as pl
from jax.experimental.pallas import tpu as pltpu
from jax.sharding import PartitionSpec as P

MESH = pl.DeviceIdType.MESH
HD = 128
EXP_SCALE = float(HD) ** (-0.5) * math.log2(math.e)
Q, K, V, O0, O1 = 0, 1, 2, 3, 4
Z_FIRST = {Q: True, K: True, V: False, O0: False, O1: False}
CHUNKS = 2
ROWS = 256 // CHUNKS


def kernel(tokens, w_qkv, w_out, listed, counts, out, wh, wo, raw, normed, queries, kv, above, below, masks, ctx_out, ctx,
           load_sem, tok_sem, recv_ring, send_ring, recv_mate, send_mate, recv_tok, send_tok, recv_tmate, send_tmate,
           recv_mask, send_mask, recv_up, recv_down, send_up, send_down, recv_edge, send_edge, recv_ctx, send_ctx,
           edge_buf, cross_buf, recv_half, send_half, recv_cross, send_cross):
    o, i = lax.axis_index("outer"), lax.axis_index("inner")
    div, rem = lax.div, lax.rem
    x, c = rem(div(o, 2), 4), rem(o, 2)
    zl, y = div(i, 4), rem(i, 4)
    zh = div(o, 8)
    z = zh * 4 + zl
    me = 2 * x + c

    def dev(x, y, z, c):
        x, y, z = rem(x + 4, 4), rem(y + 4, 4), rem(z + 8, 8)
        return (div(z, 4) * 8 + x * 2 + c, rem(z, 4) * 4 + y)

    def owner(j):
        return (zh * 8 + j, i)

    sign = 1 - 2 * c
    mate = dev(x, y, z, 1 - c)
    half, other = 4 * c, 4 * (1 - c)
    across_up = (y == 3) & (zl < 3)
    across_down = (y == 0) & (zl > 0)
    turn_up, turn_down = (c == 1) & across_up, (c == 1) & across_down
    corner_up, corner_down = (c == 1) & (y == 0) & (zl < 3), (c == 1) & (y == 3) & (zl > 0)

    tok_copy = pltpu.make_async_copy(tokens, raw, tok_sem)
    tok_copy.start()
    own_loads = {}
    for p in (K, V, Q):
        src = w_qkv.at[:, pl.ds(pl.multiple_of(1024 * p + 128 * me, 128), 128)]
        own_loads[p] = [pltpu.make_async_copy(src, wh.at[p, zl, y], load_sem.at[p])]
    for p in (O0, O1):
        own_loads[p] = []
        for k in range(2):
            r = half + 2 * (p - O0) + k
            src = w_out.at[pl.ds(pl.multiple_of(128 * r, 128), 128), :]
            own_loads[p].append(pltpu.make_async_copy(src, wo.at[r, zl, y], load_sem.at[3 + 2 * (p - O0) + k]))
    for copies in own_loads.values():
        for copy in copies:
            copy.start()

    barrier = pltpu.get_barrier_semaphore()

    def greet(device):
        pl.semaphore_signal(barrier, inc=1, device_id=device, device_id_type=MESH)

    peers = [owner(rem(me + k, 8)) for k in range(1, 8)]
    peers += [dev(x, y, z + 1, c), dev(x, y, z - 1, c), dev(x, y + 1, z, c), dev(x, y - 1, z, c),
              dev(x, y, z + 2, c), dev(x, y, z - 2, c), dev(x, y + 2, z, c), dev(x, y, z + 4, c)]
    for device in peers:
        greet(device)

    @pl.when(across_up)
    def _():
        greet(dev(x, 0, z + 1, c))

    @pl.when(across_down)
    def _():
        greet(dev(x, 3, z - 1, c))

    tok_copy.wait()

    def normalize(n, _):
        rows = pl.ds(pl.multiple_of(n * 32, 32), 32)
        values = raw[rows, :].astype(jnp.float32)
        center = values - jnp.mean(values, axis=-1, keepdims=True)
        spread = jnp.mean(center * center, axis=-1, keepdims=True)
        normed[me, rows, :] = (center * lax.rsqrt(spread + 1e-05)).astype(jnp.bfloat16)
        return 0

    lax.fori_loop(0, 8, normalize, 0)

    ids = lax.broadcasted_iota(jnp.int32, (1, 256), 1)
    for n in range(5):
        one = listed[0:1, n:n + 1]
        length = jnp.sum(jnp.where(ids == jnp.maximum(one, 0), counts[...], 0), axis=1, keepdims=True)
        masks[me, n:n + 1, :] = jnp.where((one >= 0) & (ids < length), 0.0, -jnp.inf).astype(jnp.float32)

    zero = jnp.zeros((2, 256, 128), jnp.bfloat16)
    kv[9 * zh] = zero

    @pl.when(i == 15)
    def _():
        def fill(n, _):
            above[n] = zero
            return 0
        lax.fori_loop(0, 8, fill, 0)

    @pl.when(i == 0)
    def _():
        def fill(n, _):
            below[n] = zero
            return 0
        lax.fori_loop(0, 8, fill, 0)

    def count(pred):
        return jnp.where(pred, 1, 0)

    pl.semaphore_wait(barrier, len(peers) + count(across_up) + count(across_down))

    sends = []

    def remote(src, dst, send, recv, device):
        return pltpu.make_async_remote_copy(
            src_ref=src, dst_ref=dst, send_sem=send, recv_sem=recv, device_id=device, device_id_type=MESH)

    def go(src, dst, send, recv, device):
        copy = remote(src, dst, send, recv, device)
        copy.start()
        sends.append(copy)

    def arrived(ref, recv):
        remote(ref, ref, send_mate.at[0, 0], recv, mate).wait_recv()

    here = {"z": zl, "y": y}

    def at(axis, step):
        return rem(here[axis] + step + 4, 4)

    def along(axis, step):
        return dev(x, y, z + step, c) if axis == "z" else dev(x, y + step, z, c)

    def piece(p):
        if p < O0:
            return wh.at[p]
        return wo.at[pl.ds(half + 2 * (p - O0), 2)]

    def block(p, zi, yi):
        return wh.at[p, zi, yi] if p < O0 else wo.at[pl.ds(half + 2 * (p - O0), 2), zi, yi]

    def axis_of(p, stage):
        return "z" if Z_FIRST[p] == (stage == 0) else "y"

    def part(p, stage, step):
        if stage == 0:
            return block(p, at("z", step), y) if Z_FIRST[p] else block(p, zl, at("y", step))
        return block(p, slice(None), at("y", step)) if Z_FIRST[p] else block(p, at("z", step), slice(None))

    def ring_send(p, stage, ref, slot, step):
        go(ref, ref, send_ring.at[p, stage, slot], recv_ring.at[p, stage, slot], along(axis_of(p, stage), step))

    def ring_start(p, stage, direct=False):
        ref = part(p, stage, 0)
        ring_send(p, stage, ref, 0, 1)
        ring_send(p, stage, ref, 1, -1)
        if direct:
            ring_send(p, stage, ref, 2, 2 * sign)

    def ring_relay(p, stage):
        ref = part(p, stage, -sign)
        arrived(ref, recv_ring.at[p, stage, c])
        ring_send(p, stage, ref, 2, sign)
        return ref

    def ring_finish(p, stage, direct=False):
        if direct:
            arrived(part(p, stage, -sign), recv_ring.at[p, stage, c])
        a, b = part(p, stage, sign), part(p, stage, 2)
        arrived(a, recv_ring.at[p, stage, 1 - c])
        arrived(b, recv_ring.at[p, stage, 2])
        return a, b

    def to_mate(p, n, ref):
        go(ref, ref, send_mate.at[p - O0, n], recv_mate.at[p - O0, n], mate)

    def from_mate(p):
        rows = pl.ds(other + 2 * (p - O0), 2)
        for n, step in ((0, 0), (1, sign), (2, -sign), (3, 2)):
            ref = (wo.at[rows, :, at("y", step)] if Z_FIRST[p] else wo.at[rows, at("z", step)])
            arrived(ref, recv_mate.at[p - O0, n])

    def first_start(p):
        for copy in own_loads[p]:
            copy.wait()
        ring_start(p, 0, p < O0)

    def second_start(p):
        ring_finish(p, 0, p < O0)
        ring_start(p, 1)
        if p >= O0:
            to_mate(p, 0, part(p, 1, 0))

    def second_relay(p):
        to_mate(p, 1, ring_relay(p, 1))

    def second_finish(p):
        a, b = ring_finish(p, 1)
        to_mate(p, 2, a)
        to_mate(p, 3, b)

    def rows_of(j, n):
        return normed.at[j, pl.ds(n * ROWS, ROWS)]

    def slab(step, core):
        return 2 * rem(x + step + 4, 4) + core

    def tok_start():
        evens, odds = list(range(0, CHUNKS, 2)), list(range(1, CHUNKS, 2))
        for n, m in zip(evens + odds, odds + evens):
            ref, back = rows_of(me, n), rows_of(me, m)
            go(ref, ref, send_tok.at[c, n], recv_tok.at[c, n], dev(x + sign, y, z, c))
            go(back, back, send_tok.at[1 - c, m], recv_tok.at[1 - c, m], dev(x - sign, y, z, c))
            go(ref, ref, send_tmate.at[0, n], recv_tmate.at[0, n], mate)

    def tok_relay(n):
        odd = n % 2
        way = -sign if odd else sign
        ref = rows_of(slab(-way, c), n)
        arrived(ref, recv_tok.at[1 - c if odd else c, n])
        go(ref, ref, send_tok.at[2, n], recv_tok.at[2, n], dev(x + way, y, z, c))
        go(ref, ref, send_tmate.at[1 + odd, n], recv_tmate.at[1 + odd, n], mate)

    def tok_pass(n):
        odd = n % 2
        way = -sign if odd else sign
        ref = rows_of(slab(way, c), n)
        arrived(ref, recv_tok.at[c if odd else 1 - c, n])
        go(ref, ref, send_tmate.at[2 - odd, n], recv_tmate.at[2 - odd, n], mate)

    def tok_last(n):
        ref = rows_of(slab(2, c), n)
        arrived(ref, recv_tok.at[2, n])
        go(ref, ref, send_tmate.at[3, n], recv_tmate.at[3, n], mate)

    def tok_mate(m):
        step = {0: 0, 1: sign, 2: -sign, 3: 2}[m]
        for n in range(CHUNKS):
            arrived(rows_of(slab(step, 1 - c), n), recv_tmate.at[m, n])

    conditional = []

    def when_go(pred, copy):
        @pl.when(pred)
        def _():
            copy.start()
        conditional.append((pred, copy))

    up, down = (o, jnp.minimum(i + 1, 15)), (o, jnp.maximum(i - 1, 0))
    edge_slab = 7 * (1 - zh)

    def project_kv(j):
        weights = jnp.concatenate([wh[K].reshape(2048, 128), wh[V].reshape(2048, 128)], axis=1)
        result = jnp.dot(normed[j], weights, preferred_element_type=jnp.float32).astype(jnp.bfloat16)
        kv[j + 1, 0] = result[:, :128]
        kv[j + 1, 1] = result[:, 128:]

    def halo_send(j):
        ref = kv.at[j + 1]
        when_go((i < 15) & jnp.logical_not(turn_up), remote(ref, below.at[j], send_up.at[j], recv_down.at[j], up))
        when_go((i > 0) & jnp.logical_not(turn_down), remote(ref, above.at[j], send_down.at[j], recv_up.at[j], down))
        when_go(turn_up, remote(ref, cross_buf.at[j], send_up.at[j], recv_cross.at[j], dev(x, y + 1, z, c)))
        when_go(turn_down, remote(ref, cross_buf.at[j], send_down.at[j], recv_cross.at[j], dev(x, y - 1, z, c)))
        when_go(j == edge_slab, remote(ref, kv.at[9 * zh], send_edge, recv_edge, dev(x, y, z + 4, c)))

    def cross_relay(j):
        ref = cross_buf.at[j]

        @pl.when(corner_up | corner_down)
        def _():
            arrived(ref, recv_cross.at[j])
        when_go(corner_up, remote(ref, below.at[j], send_cross.at[j], recv_down.at[j], dev(x, y, z + 1, c)))
        when_go(corner_down, remote(ref, above.at[j], send_cross.at[j], recv_up.at[j], dev(x, y, z - 1, c)))

    end = rem(z + 2 * sign + 8, 8)

    def edge_relay(pred):
        @pl.when(pred)
        def _():
            arrived(edge_buf, recv_half)
        when_go(pred, remote(edge_buf, kv.at[9 * (1 - div(end, 4))], send_edge, recv_edge, dev(x, y, end, c)))

    outer_x = (x == 0) | (x == 3)

    def project_q(j):
        queries[j] = jnp.dot(normed[j], wh[Q].reshape(2048, 128), preferred_element_type=jnp.float32).astype(jnp.bfloat16)

    def attend(j, target):
        @pl.when(i < 15)
        def _():
            arrived(above.at[j], recv_up.at[j])

        @pl.when(i > 0)
        def _():
            arrived(below.at[j], recv_down.at[j])

        @pl.when(j == edge_slab)
        def _():
            arrived(kv.at[9 * (1 - zh)], recv_edge)

        query = queries[j]
        pairs = (lambda n: kv[j + 1, n], lambda n: kv[j, n], lambda n: kv[j + 2, n], lambda n: below[j, n],
                 lambda n: above[j, n])
        scores = []
        for n in range(5):
            s = lax.dot_general(query, pairs[n](0), (((1,), (1,)), ((), ())), preferred_element_type=jnp.float32)
            scores.append(s + masks[j, n:n + 1, :])
        top = scores[0]
        for n in range(1, 5):
            top = jnp.maximum(top, scores[n])
        largest = jnp.max(top, axis=1, keepdims=True)
        total = None
        acc = None
        for n in range(5):
            weight = jnp.exp2((scores[n] - largest) * EXP_SCALE)
            total = weight if total is None else total + weight
            one = jnp.dot(weight.astype(jnp.bfloat16), pairs[n](1), preferred_element_type=jnp.float32)
            acc = one if acc is None else acc + one
        totals = jnp.sum(total, axis=1, keepdims=True)
        target[...] = (acc / totals).astype(jnp.bfloat16)

    def attend_send(j):
        attend(j, ctx_out.at[j])
        go(ctx_out.at[j], ctx.at[me], send_ctx.at[j], recv_ctx.at[me], owner(j))

    def out_project():
        left = jnp.concatenate([ctx[h] for h in range(8)], axis=1)

        def body(n, _):
            zz, yy = div(n, 2), 2 * rem(n, 2)
            weights = jnp.concatenate(
                [wo[:, zz, yy].reshape(1024, 128), wo[:, zz, yy + 1].reshape(1024, 128)], axis=1)
            result = jnp.dot(left, weights, preferred_element_type=jnp.float32)
            out[:, pl.ds(pl.multiple_of(n * 256, 256), 256)] = result.astype(jnp.bfloat16)
            return 0

        lax.fori_loop(0, 8, body, 0)

    own, pal = me, slab(0, 1 - c)
    near = [slab(-sign, c), slab(sign, 1 - c), slab(sign, c), slab(-sign, 1 - c)]
    far = [slab(2, c), slab(2, 1 - c)]

    def handle(j):
        project_kv(j)
        halo_send(j)

    tok_start()
    for k in range(1, 8):
        go(masks.at[me], masks.at[me], send_mask.at[k], recv_mask.at[me], owner(rem(me + k, 8)))
    for p in (K, V, Q, O0, O1):
        first_start(p)
    for p in (K, V, Q):
        second_start(p)
    for p in (O0, O1):
        ring_relay(p, 0)
    for p in (K, V, Q):
        ring_relay(p, 1)
    for p in (O0, O1):
        second_start(p)
    tok_relay(0)
    for p in (K, V):
        ring_finish(p, 1)
    handle(own)
    tok_mate(0)
    handle(pal)
    for n in range(1, CHUNKS):
        tok_relay(n)
    cross_relay(own)
    cross_relay(pal)
    for n in range(CHUNKS):
        tok_pass(n)
    for p in (O0, O1):
        second_relay(p)
    ring_finish(Q, 1)
    handle(near[0])
    handle(near[2])
    tok_mate(1)
    handle(near[1])
    tok_mate(2)
    handle(near[3])
    for p in (O0, O1):
        second_finish(p)
    project_q(own)
    project_q(pal)
    for j in (near[0], near[2], near[1], near[3]):
        cross_relay(j)
    for n in range(CHUNKS):
        tok_last(n)
    for k in range(1, 8):
        j = rem(me + k, 8)
        arrived(masks.at[j], recv_mask.at[j])
    handle(far[0])
    tok_mate(3)
    handle(far[1])
    attend(own, ctx.at[me])
    attend_send(pal)
    for j in far:
        cross_relay(j)
    for j in near:
        project_q(j)
    for j in near:
        attend_send(j)
    for j in far:
        project_q(j)
    for j in far:
        attend_send(j)
    for p in (O0, O1):
        from_mate(p)
    for k in range(1, 8):
        j = rem(me + k, 8)
        arrived(ctx.at[j], recv_ctx.at[j])
    out_project()
    for copy in sends:
        copy.wait_send()
    for pred, copy in conditional:
        @pl.when(pred)
        def _(copy=copy):
            copy.wait_send()


def per_device(tokens, w_qkv, w_out, neighbours, counts):
    dma = pltpu.SemaphoreType.DMA
    vmem, hbm = pl.BlockSpec(memory_space=pltpu.VMEM), pl.BlockSpec(memory_space=pl.ANY)
    bf16 = jnp.bfloat16
    return pl.pallas_call(
        kernel,
        out_shape=jax.ShapeDtypeStruct((256, 2048), bf16),
        in_specs=[hbm, hbm, hbm, vmem, vmem],
        out_specs=vmem,
        scratch_shapes=[
            pltpu.VMEM((3, 4, 4, 128, 128), bf16),
            pltpu.VMEM((8, 4, 4, 128, 128), bf16),
            pltpu.VMEM((256, 2048), bf16),
            pltpu.VMEM((8, 256, 2048), bf16),
            pltpu.VMEM((8, 256, 128), bf16),
            pltpu.VMEM((10, 2, 256, 128), bf16),
            pltpu.VMEM((8, 2, 256, 128), bf16),
            pltpu.VMEM((8, 2, 256, 128), bf16),
            pltpu.VMEM((8, 8, 256), jnp.float32),
            pltpu.VMEM((8, 256, 128), bf16),
            pltpu.VMEM((8, 256, 128), bf16),
            dma((7,)), dma,
            dma((5, 2, 3)), dma((5, 2, 3)),
            dma((2, 4)), dma((2, 4)),
            dma((3, CHUNKS)), dma((3, CHUNKS)),
            dma((4, CHUNKS)), dma((4, CHUNKS)),
            dma((8,)), dma((8,)),
            dma((8,)), dma((8,)), dma((8,)), dma((8,)),
            dma, dma,
            dma((8,)), dma((8,)),
            pltpu.VMEM((2, 256, 128), bf16),
            pltpu.VMEM((8, 2, 256, 128), bf16),
            dma, dma,
            dma((8,)), dma((8,)),
        ],
        compiler_params=pltpu.CompilerParams(
            collective_id=0, has_side_effects=True, vmem_limit_bytes=60 << 20),
    )(tokens, w_qkv, w_out, neighbours, counts.reshape(1, 256))


def solution(mesh):
    placed = (P(("outer", "inner"), None), P("inner", None), P(None, "inner"), P(("outer", "inner"), None), P())
    return jax.shard_map(
        per_device, mesh=mesh, in_specs=placed, out_specs=P(("outer", "inner"), None), check_vma=False)
```
